32 devices in a mesh: gx: 8 (over z, x), gy: 4 (over y, core).
Axes of the slice: x: 2, y: 2, z: 4, core: 2. Of those that a mesh axis runs over, the one named last changes fastest.
Arguments:
- self_blk: float32 [64, 128, 128], P(('gx', 'gy')), may hold values from -6 to 6
- near: bfloat16 [64, 14, 512, 128], P(('gx', 'gy')), may hold values from -0.59765625 to 0.59765625
- back: bfloat16 [64, 14, 128, 512], P(('gx', 'gy')), may hold values from -0.59765625 to 0.59765625
- interp: bfloat16 [64, 128, 512], P(('gx', 'gy')), may hold values from -0.59765625 to 0.59765625
- redinv: bfloat16 [64, 512, 512], P(('gx', 'gy')), as said below
- ranks: int32 [64], P(('gx', 'gy')), may hold values from 64 to 128, as said below
- pivots: int32 [64, 128], P(('gx', 'gy')), may hold values from 0 to 511, as said below
- neighbors: int32 [64, 14], P(('gx', 'gy')), may hold values from 0 to 63, as said below
- parent: int32 [64], P(('gx', 'gy')), may hold values from 0 to 63, as said below
Outputs:
- parent_blocks: float32 [64, 128, 128], P(('gx', 'gy'))
The draws below stay inside these ranges and needn't reach their ends.
Inputs may be any that keep to these rules, and one draw needn't show every extreme that they name: redinv is used only on a box's redundant points. `ranks`: every draw has a box of rank 128 and a box of rank 64. `pivots`: the 128 entries of a box are distinct; the first ranks[b] of them are its skeleton points, the others are redundant points. `neighbors`: box b lies on the device of linear index b // 2, gx major. A box's neighbours are distinct, never the box itself, and lie on devices of the same gy index. The entries of the 2 boxes of one device name boxes of any one device at most 4 times; in every draw and every gy index one device is named exactly 4 times by each other device of that gy index. `parent`: A permutation of the boxes that maps the 8 boxes of each gx index onto the same 8 rows.
All inputs are finite; a program needn't handle non-finite values.
Results may differ from the reference program's by a relative error of at most 0.0049.
Values may be sent and summed in bfloat16 or wider, within the bound.
No kernel may reach another device: no remote copies, remote signals or barrier semaphores. Data moves between devices by JAX's collectives and lax.ppermute only.
A program may use at most 64 MiB of HBM per device.

```python
import math
import jax
import jax.numpy as jnp
from jax import lax

P_SIZE = 512
K = 128
NB = 14
BOX_DEV = 2
KMIN = 64
PEERS = 8
LANES = 4
ROW_BOXES = 8
BOXES = 64


def draw_redinv(key, part):
    sub = jax.random.fold_in(key, 15)
    noise = 0.5 * jax.random.normal(sub, (BOXES, P_SIZE, P_SIZE), jnp.float32)
    full = jnp.eye(P_SIZE, dtype=jnp.float32)[None] + noise / math.sqrt(P_SIZE)
    return full.astype(jnp.bfloat16)


def draw_ranks(key, part):
    base = jax.random.fold_in(key, 11)
    values = jax.random.randint(jax.random.fold_in(base, 1), (BOXES,), KMIN, K + 1)
    highest = jax.random.randint(jax.random.fold_in(base, 2), (), 0, BOXES)
    lowest = (highest + 1 + jax.random.randint(jax.random.fold_in(base, 3), (), 0, BOXES - 1)) % BOXES
    values = values.at[highest].set(K)
    values = values.at[lowest].set(KMIN)
    return values.astype(jnp.int32)


def draw_pivots(key, part):
    keys = jax.random.split(jax.random.fold_in(key, 12), BOXES)

    def one_box(sub):
        return jax.random.permutation(sub, P_SIZE)[:K]
    return jax.vmap(one_box)(keys).astype(jnp.int32)


def draw_neighbors(key, part):
    base = jax.random.fold_in(key, 13)
    hottest = jax.random.randint(jax.random.fold_in(base, 1), (LANES,), 0, PEERS)
    keys = jax.random.split(jax.random.fold_in(base, 2), BOXES)
    column = PEERS * BOX_DEV
    candidates = jnp.arange(column, dtype=jnp.int32)

    def one_box(sub, box):
        device = box // BOX_DEV
        slot = box % BOX_DEV
        gx_row = device // LANES
        lane = device % LANES
        first_key, second_key = jax.random.split(sub)
        scores = jax.random.permutation(first_key, column).astype(jnp.int32)
        on_hot = candidates // BOX_DEV == hottest[lane]
        scores = jnp.where(on_hot, -1, scores)
        scores = jnp.where(candidates == gx_row * BOX_DEV + slot, column + 1, scores)
        ordered = jnp.argsort(scores, stable=True)[:NB]
        mixing = jax.random.permutation(second_key, NB)
        chosen = ordered[mixing].astype(jnp.int32)
        target_device = chosen // BOX_DEV * LANES + lane
        return (target_device * BOX_DEV + chosen % BOX_DEV).astype(jnp.int32)
    return jax.vmap(one_box)(keys, jnp.arange(BOXES, dtype=jnp.int32))


def draw_parent(key, part):
    keys = jax.random.split(jax.random.fold_in(key, 14), PEERS)

    def one_row(sub):
        return jax.random.permutation(sub, ROW_BOXES).astype(jnp.int32)
    perms = jax.vmap(one_row)(keys)
    offsets = (jnp.arange(PEERS, dtype=jnp.int32) * ROW_BOXES)[:, None]
    return (perms + offsets).reshape(BOXES).astype(jnp.int32)


def level_of(key, extent, cuts, low, largest):
    gain = 1.0
    for position, parts in cuts:
        steps = jax.random.uniform(jax.random.fold_in(jax.random.fold_in(key, 6), position), (parts,), jnp.float32, low / len(cuts), largest / len(cuts))
        gain = gain * jnp.repeat(jnp.exp(steps), extent[position] // parts).reshape((-1,) + (1,) * (len(extent) - 1 - position))
    return gain


def normal_values(key, shape, scale, reach, pieces=(), kind=jnp.bfloat16):
    drawn = scale * jax.random.normal(key, shape, jnp.float32)
    if pieces:
        drawn = drawn * level_of(key, shape, pieces, -0.22, 0.18)
    return jnp.clip(drawn, -reach, reach).astype(kind)


def setup_inputs(seed: int = 0) -> dict:
    seeds = jax.random.split(jax.random.key(seed), 10)
    return {
        "self_blk": normal_values(seeds[0], (BOXES, K, K), 1.0, 6.0, ((0, 32),), jnp.float32),
        "near": normal_values(seeds[1], (BOXES, NB, P_SIZE, K), 0.1, 0.59765625, ((0, 32),)),
        "back": normal_values(seeds[2], (BOXES, NB, K, P_SIZE), 0.1, 0.59765625, ((0, 32),)),
        "interp": normal_values(seeds[3], (BOXES, K, P_SIZE), 0.1, 0.59765625, ((0, 32),)),
        "redinv": draw_redinv(jax.random.fold_in(seeds[9], 71), 0),
        "ranks": draw_ranks(jax.random.fold_in(seeds[9], 71), 0),
        "pivots": draw_pivots(jax.random.fold_in(seeds[9], 71), 0),
        "neighbors": draw_neighbors(jax.random.fold_in(seeds[9], 71), 0),
        "parent": draw_parent(jax.random.fold_in(seeds[9], 71), 0),
    }


def box_updates(near_b, back_b, interp_b, redinv_b, rank_b, pivot_b):
    points = jnp.arange(P_SIZE, dtype=jnp.int32)
    living = jnp.arange(K, dtype=jnp.int32) < rank_b
    select = jnp.where((pivot_b[:, None] == points[None, :]) & living[:, None], 1.0, 0.0).astype(jnp.float32)
    redundant = 1.0 - jnp.sum(select, axis=0)
    alive_rows = jnp.where(living, 1.0, 0.0).astype(jnp.float32)
    coefficients = interp_b.astype(jnp.float32) * alive_rows[:, None] * redundant[None, :]
    placed = jnp.dot(coefficients.T, select, precision=lax.Precision.HIGHEST)
    compress = (redundant[:, None] * (jnp.eye(P_SIZE, dtype=jnp.float32) - placed)).astype(jnp.bfloat16)
    halfway = jnp.dot(redinv_b, compress, preferred_element_type=jnp.float32).astype(jnp.bfloat16)
    eliminator = jnp.dot(compress.T, halfway, preferred_element_type=jnp.float32).astype(jnp.bfloat16)
    lifted = jnp.einsum('nkp,pq->nkq', back_b.astype(jnp.float32), eliminator.astype(jnp.float32),
                        precision=lax.Precision.HIGHEST).astype(jnp.bfloat16)
    lifted = lax.optimization_barrier(lifted)
    return -jnp.einsum('nkq,nql->nkl', lifted.astype(jnp.float32), near_b.astype(jnp.float32),
                       precision=lax.Precision.HIGHEST)


def reference(self_blk, near, back, interp, redinv, ranks, pivots, neighbors, parent):
    device_total = BOXES // BOX_DEV
    entry_count = BOX_DEV * NB

    def device_step(summed, device_index):
        first_box = (device_index * BOX_DEV).astype(jnp.int32)

        def window(array):
            return lax.dynamic_slice_in_dim(array, first_box, BOX_DEV, 0)

        updates = jax.vmap(box_updates)(window(near), window(back), window(interp), window(redinv),
                                        window(ranks), window(pivots))
        flattened = updates.reshape(entry_count, K * K)
        targets = window(neighbors).reshape(entry_count)
        same_target = jnp.where(targets[:, None] == targets[None, :], 1.0, 0.0).astype(jnp.float32)
        grouped = jnp.dot(same_target, flattened, precision=lax.Precision.HIGHEST).astype(jnp.bfloat16)
        grouped = lax.optimization_barrier(grouped)
        earlier = jnp.sum(jnp.tril(same_target, -1), axis=1)
        leading = jnp.where(earlier == 0.0, 1.0, 0.0).astype(jnp.float32)
        summed = summed.at[targets].add(grouped.astype(jnp.float32) * leading[:, None])
        return summed, None

    summed, unused = lax.scan(device_step, jnp.zeros((BOXES, K * K), jnp.float32),
                              jnp.arange(device_total, dtype=jnp.int32))
    living = jnp.arange(K, dtype=jnp.int32)[None, :] < ranks[:, None]
    masking = living[:, :, None] & living[:, None, :]
    schur = jnp.where(masking, self_blk + summed.reshape(BOXES, K, K), 0.0)
    return jnp.zeros_like(schur).at[parent].set(schur)
```

```python
import jax
import jax.numpy as jnp
from jax import lax
from jax.experimental import pallas as pl
from jax.experimental.pallas import tpu as pltpu
from jax.sharding import PartitionSpec as P

GX = "gx"
GY = "gy"


def nt(a, b):
    return lax.dot_general(a, b, (((1,), (1,)), ((), ())), preferred_element_type=jnp.float32)


def nn(a, b):
    return jnp.dot(a, b, preferred_element_type=jnp.float32)


def eliminator_of(interp, redinv, pivot_row, rank):
    width, points = interp.shape
    point_col = lax.broadcasted_iota(jnp.int32, (points, width), 0)
    skel_row = lax.broadcasted_iota(jnp.int32, (points, width), 1)
    hit = (point_col == pivot_row) & (skel_row < rank)
    select_t = jnp.where(hit, 1.0, 0.0).astype(jnp.bfloat16)
    ones = jnp.ones((8, width), jnp.bfloat16)
    chosen_row = nt(ones, select_t)[:1]
    redundant_row = chosen_row < 0.5
    redundant_col = jnp.max(jnp.where(hit, 1.0, 0.0), axis=1, keepdims=True) < 0.5
    living = lax.broadcasted_iota(jnp.int32, (width, points), 0) < rank
    coefficients = jnp.where(living & redundant_row, interp, jnp.zeros_like(interp))
    half_skel = (-nt(redinv, coefficients)).astype(jnp.bfloat16)
    halfway = jnp.where(redundant_row, redinv, nt(half_skel, select_t).astype(jnp.bfloat16))
    elim_skel = (-nn(coefficients, halfway)).astype(jnp.bfloat16)
    return jnp.where(redundant_col, halfway, nn(select_t, elim_skel).astype(jnp.bfloat16))


def make_kernel(box_dev, near_count, gx_count, lane_count, width, points, parts):
    def kernel(ranks, neighbors, pivots, interp_hbm, redinv_hbm, back_hbm, near_hbm, *rest):
        outs = rest[:gx_count]
        interp_v, redinv_v, back_v, near_v, lifted_v, table, sems = rest[gx_count:]
        per = near_count // parts
        small, bulk = [], []
        for b in range(box_dev):
            small.append(
                (
                    pltpu.make_async_copy(interp_hbm.at[b], interp_v.at[b], sems.at[b, 0]),
                    pltpu.make_async_copy(redinv_hbm.at[b], redinv_v.at[b], sems.at[b, 1]),
                )
            )
        for b in range(box_dev):
            copies = []
            for c in range(parts):
                part = pl.ds(c * per, per)
                copies.append(
                    pltpu.make_async_copy(
                        back_hbm.at[b, part], back_v.at[b, part], sems.at[b, 3 + c]
                    )
                )
            bulk.append(copies)
        near_copies = [
            pltpu.make_async_copy(near_hbm.at[b], near_v.at[b], sems.at[b, 2])
            for b in range(box_dev)
        ]
        for pair in small:
            pair[0].start()
            pair[1].start()
        for copies in bulk:
            for copy in copies:
                copy.start()
        for copy in near_copies:
            copy.start()
        me = lax.axis_index(GX)
        for b in range(box_dev):
            for u in range(gx_count * box_dev):
                table[b, u] = near_count
        for b in range(box_dev):
            for n in range(near_count):
                target = neighbors[b, n]
                row = target // (box_dev * lane_count)
                table[b, (row ^ me) * box_dev + target % box_dev] = n
            lifted_v[b, near_count] = jnp.zeros((width, points), jnp.bfloat16)
        elims = []
        for b in range(box_dev):
            small[b][0].wait()
            small[b][1].wait()
            elims.append(
                eliminator_of(interp_v[b], redinv_v[b], pivots[pl.ds(b, 1), :], ranks[b])
            )
        for b in range(box_dev):
            for c in range(parts):
                bulk[b][c].wait()
                rows = back_v[b, pl.ds(c * per, per)].reshape(per * width, points)
                lifted_v[b, pl.ds(c * per, per)] = (
                    nn(rows, elims[b]).astype(jnp.bfloat16).reshape(per, width, points)
                )
        for copy in near_copies:
            copy.wait()
        for k in range(gx_count):
            for s in range(box_dev):
                total = None
                for b in range(box_dev):
                    n = table[b, k * box_dev + s]
                    term = nn(lifted_v[b, n], near_v[b, jnp.minimum(n, near_count - 1)])
                    total = term if total is None else total + term
                outs[k][s] = (-total).astype(jnp.bfloat16)

    return kernel


def local_updates(near, back, interp, redinv, ranks, pivots, neighbors):
    box_dev, near_count, points, width = near.shape
    gx_count = lax.axis_size(GX)
    lane_count = lax.axis_size(GY)
    parts = 2 if near_count % 2 == 0 else 1
    kernel = make_kernel(box_dev, near_count, gx_count, lane_count, width, points, parts)
    smem = pl.BlockSpec(memory_space=pltpu.SMEM)
    vmem = pl.BlockSpec(memory_space=pltpu.VMEM)
    anywhere = pl.BlockSpec(memory_space=pl.ANY)
    bf16 = jnp.bfloat16
    return pl.pallas_call(
        kernel,
        out_shape=[jax.ShapeDtypeStruct((box_dev, width, width), bf16)] * gx_count,
        in_specs=[smem, smem, vmem, anywhere, anywhere, anywhere, anywhere],
        out_specs=[vmem] * gx_count,
        scratch_shapes=[
            pltpu.VMEM((box_dev, width, points), bf16),
            pltpu.VMEM((box_dev, points, points), bf16),
            pltpu.VMEM((box_dev, near_count, width, points), bf16),
            pltpu.VMEM((box_dev, near_count, points, width), bf16),
            pltpu.VMEM((box_dev, near_count + 1, width, points), bf16),
            pltpu.SMEM((box_dev, gx_count * box_dev), jnp.int32),
            pltpu.SemaphoreType.DMA((box_dev, 3 + parts)),
        ],
        compiler_params=pltpu.CompilerParams(vmem_limit_bytes=40 * 1024 * 1024),
        name="updates",
    )(ranks, neighbors, pivots, interp, redinv, back, near)


def swap(value, axis, size, k):
    return lax.ppermute(value, axis, [(a, a ^ k) for a in range(size)])


def body(self_blk, near, back, interp, redinv, ranks, pivots, neighbors, parent):
    gx_count = lax.axis_size(GX)
    lane_count = lax.axis_size(GY)
    box_dev, width = self_blk.shape[:2]
    parts = local_updates(near, back, interp, redinv, ranks, pivots, neighbors)
    arrived = [parts[0]]
    for k in range(1, gx_count):
        arrived.append(swap(parts[k], GX, gx_count, k))
    summed = sum(a.astype(jnp.float32) for a in arrived)
    living = jnp.arange(width, dtype=jnp.int32)[None, :] < ranks[:, None]
    masking = living[:, :, None] & living[:, None, :]
    merged = jnp.where(masking, self_blk + summed, 0.0)
    row = parent - lax.axis_index(GX) * (lane_count * box_dev)
    lane = lax.axis_index(GY)
    result = None
    for k in range(lane_count):
        slots = []
        for s in range(box_dev):
            here = row == (lane ^ k) * box_dev + s
            slots.append(jnp.sum(jnp.where(here[:, None, None], merged, 0.0), axis=0))
        placed = jnp.stack(slots)
        if k:
            placed = swap(placed.astype(jnp.bfloat16), GY, lane_count, k).astype(jnp.float32)
        result = placed if result is None else result + placed
    return result


def solution(mesh):
    split = (GX, GY)
    placed = (
        P(split, None, None),
        P(split, None, None, None),
        P(split, None, None, None),
        P(split, None, None),
        P(split, None, None),
        P(split),
        P(split, None),
        P(split, None),
        P(split),
    )
    return jax.shard_map(
        body, mesh=mesh, in_specs=placed, out_specs=P(split, None, None), check_vma=False
    )
```

```python
import jax
import jax.numpy as jnp
from jax import lax
from jax.experimental import pallas as pl
from jax.experimental.pallas import tpu as pltpu
from jax.sharding import PartitionSpec as P


GX = "gx"
GY = "gy"


def nt(a, b):
    return lax.dot_general(a, b, (((1,), (1,)), ((), ())), preferred_element_type=jnp.float32)


def nn(a, b):
    return jnp.dot(a, b, preferred_element_type=jnp.float32)


def eliminator_of(interp, redinv, pivot_row, rank):
    width, points = interp.shape
    pivot_col = jnp.transpose(jnp.broadcast_to(pivot_row, (8, width)))[:, :1]
    slot = lax.broadcasted_iota(jnp.int32, (width, points), 0)
    point = lax.broadcasted_iota(jnp.int32, (width, points), 1)
    select = jnp.where((point == pivot_col) & (slot < rank), 1.0, 0.0)
    redundant_row = jnp.sum(select, axis=0, keepdims=True) < 0.5
    slot_t = lax.broadcasted_iota(jnp.int32, (points, width), 1)
    point_t = lax.broadcasted_iota(jnp.int32, (points, width), 0)
    select_t = jnp.where((point_t == pivot_row) & (slot_t < rank), 1.0, 0.0)
    redundant_col = jnp.max(select_t, axis=1, keepdims=True) < 0.5
    coefficients = jnp.where((slot < rank) & redundant_row, interp, jnp.zeros_like(interp))
    half_skel = (-nt(redinv, coefficients)).astype(jnp.bfloat16)
    spread = nn(half_skel, select.astype(jnp.bfloat16)).astype(jnp.bfloat16)
    halfway = jnp.where(redundant_row, redinv, spread)
    elim_skel = (-nn(coefficients, halfway)).astype(jnp.bfloat16)
    spread = nn(select_t.astype(jnp.bfloat16), elim_skel).astype(jnp.bfloat16)
    return jnp.where(redundant_col, halfway, spread)


def fill_table(table, neighbors, box_dev, near_count, lane_count, slots):
    me = lax.axis_index(GX)
    for b in range(box_dev):
        for u in range(slots):
            table[b, u] = near_count
    for b in range(box_dev):
        for n in range(near_count):
            target = neighbors[b, n]
            row = target // (box_dev * lane_count)
            table[b, (row ^ me) * box_dev + target % box_dev] = n


def slot_updates(table, slots, elims, back_v, near_v, lifted_v, near_count, group, store, ready=None):
    box_dev, _, width, _ = back_v.shape
    for first in range(0, len(slots), group):
        these = slots[first : first + group]
        for b in range(box_dev):
            rows = jnp.concatenate([back_v[b, table[b, u]] for u in these], axis=0)
            lifted_v[b, pl.ds(0, len(these) * width)] = nn(rows, elims[b][...]).astype(jnp.bfloat16)
        if ready is not None and first == 0:
            ready()
        for i, u in enumerate(these):
            total = None
            for b in range(box_dev):
                if u != b:
                    n = jnp.minimum(table[b, u], near_count - 1)
                    term = nn(lifted_v[b, pl.ds(i * width, width)], near_v[b, n])
                    total = term if total is None else total + term
            store(first + i, (-total).astype(jnp.bfloat16))


def early_kernel(sizes, early):
    box_dev, near_count, lane_count, slots, group = sizes

    def kernel(ranks_h, neighbors_h, pivots_h, interp_h, redinv_h, back_h, near_h, *rest):
        out, elim_v, ranks, neighbors, pivots, interp_v, redinv_v, back_v, near_v = rest[:9]
        lifted_v, table, few, sems = rest[9:]
        width, points = interp_v.shape[1:]
        heads = [
            pltpu.make_async_copy(neighbors_h, neighbors, few.at[0]),
            pltpu.make_async_copy(ranks_h, ranks, few.at[1]),
            pltpu.make_async_copy(pivots_h, pivots, few.at[2]),
        ]
        copies = []
        for b in range(box_dev):
            copies.append(
                [
                    pltpu.make_async_copy(interp_h.at[b], interp_v.at[b], sems.at[b, 0]),
                    pltpu.make_async_copy(redinv_h.at[b], redinv_v.at[b], sems.at[b, 1]),
                    pltpu.make_async_copy(
                        back_h.at[b], back_v.at[b, pl.ds(0, near_count)], sems.at[b, 2]
                    ),
                    pltpu.make_async_copy(near_h.at[b], near_v.at[b], sems.at[b, 3]),
                ]
            )
        for copy in heads:
            copy.start()
        for b in range(box_dev):
            copies[b][0].start()
            copies[b][1].start()
        for b in range(box_dev):
            back_v[b, near_count] = jnp.zeros((width, points), jnp.bfloat16)
        for copy in heads:
            copy.wait()
        fill_table(table, neighbors, box_dev, near_count, lane_count, slots)
        elims = []
        for b in range(box_dev):
            copies[b][0].wait()
            copies[b][1].wait()
            if b == 0:
                for j in (2, 3):
                    for c in range(box_dev):
                        copies[c][j].start()
        for b in range(box_dev):
            elim_v[b] = eliminator_of(interp_v[b], redinv_v[b], pivots[pl.ds(b, 1), :], ranks[b])
            elims.append(elim_v.at[b])
        for b in range(box_dev):
            copies[b][2].wait()

        def store(i, block):
            out[i] = block

        slot_updates(table, early, elims, back_v, near_v, lifted_v, near_count, group, store, lambda: [copies[b][3].wait() for b in range(box_dev)])

    return kernel


def late_kernel(sizes, late, splits):
    box_dev, near_count, lane_count, slots = sizes[:4]

    def kernel(neighbors_h, back_h, near_h, elim_v, *rest):
        outs = rest[:-8]
        neighbors, back_v, near_v, lifted_v, table, few, back_sems, near_sems = rest[-8:]
        width, points = back_v.shape[2:]
        head = pltpu.make_async_copy(neighbors_h, neighbors, few.at[0])
        head.start()
        spans = [pl.ds(first, count) for first, count in splits]
        back_copies = [
            [
                pltpu.make_async_copy(
                    back_h.at[b, span], back_v.at[b, span], back_sems.at[b, i]
                )
                for b in range(box_dev)
            ]
            for i, span in enumerate(spans)
        ]
        near_copies = [
            pltpu.make_async_copy(near_h.at[b], near_v.at[b], near_sems.at[b])
            for b in range(box_dev)
        ]
        for copies in back_copies + [near_copies]:
            for copy in copies:
                copy.start()
        for b in range(box_dev):
            lifted_v[b, near_count] = jnp.zeros((width, points), jnp.bfloat16)
        head.wait()
        fill_table(table, neighbors, box_dev, near_count, lane_count, slots)
        for (first, count), span, copies in zip(splits, spans, back_copies):
            for copy in copies:
                copy.wait()
            for b in range(box_dev):
                rows = back_v[b, span].reshape(count * width, points)
                lifted = nn(rows, elim_v[b]).astype(jnp.bfloat16)
                lifted_v[b, span] = lifted.reshape(count, width, points)
        for copy in near_copies:
            copy.wait()
        for i, u in enumerate(late):
            total = None
            for b in range(box_dev):
                if u != b:
                    n = table[b, u]
                    term = nn(lifted_v[b, n], near_v[b, jnp.minimum(n, near_count - 1)])
                    total = term if total is None else total + term
            outs[i // box_dev][i % box_dev] = (-total).astype(jnp.bfloat16)

    return kernel


def in_hbm(*values):
    return [pltpu.with_memory_space_constraint(v, pltpu.HBM) for v in values]


def swap(value, axis, size, k):
    return lax.ppermute(value, axis, [(a, a ^ k) for a in range(size)])


def layer(self_blk, near, back, interp, redinv, ranks, pivots, neighbors, parent):
    gx_count = lax.axis_size(GX)
    lane_count = lax.axis_size(GY)
    box_dev, near_count, points, width = near.shape
    bf16 = jnp.bfloat16
    half, quarter = gx_count // 2, gx_count // 4
    early_k = [half + quarter + j for j in range(quarter)]
    late_k = [half + j for j in range(quarter)] + list(range(half))
    group = 4
    sizes = (box_dev, near_count, lane_count, gx_count * box_dev, group)
    slots_of = lambda ks: [k * box_dev + s for k in ks for s in range(box_dev)]
    hbm = pl.BlockSpec(memory_space=pltpu.HBM)
    vmem = pl.BlockSpec(memory_space=pltpu.VMEM)
    table = pltpu.SMEM((box_dev, gx_count * box_dev), jnp.int32)
    params = pltpu.CompilerParams(vmem_limit_bytes=24 * 1024 * 1024)
    early, elim = pl.pallas_call(
        early_kernel(sizes, slots_of(early_k)),
        out_shape=[
            jax.ShapeDtypeStruct((len(early_k) * box_dev, width, width), bf16),
            jax.ShapeDtypeStruct((box_dev, points, points), bf16),
        ],
        in_specs=[hbm] * 7,
        out_specs=[vmem] * 2,
        scratch_shapes=[
            pltpu.SMEM((box_dev,), jnp.int32),
            pltpu.SMEM((box_dev, near_count), jnp.int32),
            pltpu.VMEM((box_dev, width), jnp.int32),
            pltpu.VMEM(interp.shape, bf16),
            pltpu.VMEM(redinv.shape, bf16),
            pltpu.VMEM((box_dev, near_count + 1, width, points), bf16),
            pltpu.VMEM(near.shape, bf16),
            pltpu.VMEM((box_dev, group * width, points), bf16),
            table,
            pltpu.SemaphoreType.DMA((3,)),
            pltpu.SemaphoreType.DMA((box_dev, 4)),
        ],
        compiler_params=params,
        name="early",
    )(*in_hbm(ranks, neighbors, pivots, interp, redinv, back, near))
    joined = swap(early, GX, gx_count, quarter)
    split = near_count // 2
    splits = [(0, split), (split, near_count - split)]
    late = pl.pallas_call(
        late_kernel(sizes, slots_of(late_k), splits),
        out_shape=[jax.ShapeDtypeStruct((box_dev, width, width), bf16)] * len(late_k),
        in_specs=[hbm] * 3 + [vmem],
        out_specs=[vmem] * len(late_k),
        scratch_shapes=[
            pltpu.SMEM((box_dev, near_count), jnp.int32),
            pltpu.VMEM(back.shape, bf16),
            pltpu.VMEM(near.shape, bf16),
            pltpu.VMEM((box_dev, near_count + 1, width, points), bf16),
            table,
            pltpu.SemaphoreType.DMA((1,)),
            pltpu.SemaphoreType.DMA((box_dev, len(splits))),
            pltpu.SemaphoreType.DMA((box_dev,)),
        ],
        compiler_params=params,
        name="late",
    )(*in_hbm(neighbors, back, near), elim)
    part = dict(zip(late_k, late))
    summed = part[0].astype(jnp.float32)
    for j in reversed(range(quarter)):
        k = half + j
        added = joined[j * box_dev : (j + 1) * box_dev].astype(jnp.float32)
        block = (part[k].astype(jnp.float32) + added).astype(bf16)
        summed += swap(block, GX, gx_count, k).astype(jnp.float32)
    for k in reversed(range(1, half)):
        summed += swap(part[k], GX, gx_count, k).astype(jnp.float32)
    living = jnp.arange(width, dtype=jnp.int32)[None, :] < ranks[:, None]
    masking = living[:, :, None] & living[:, None, :]
    merged = jnp.where(masking, self_blk + summed, 0.0)
    row = parent - lax.axis_index(GX) * (lane_count * box_dev)
    lane = lax.axis_index(GY)
    result = None
    for k in range(lane_count):
        rows = []
        for s in range(box_dev):
            here = row == (lane ^ k) * box_dev + s
            rows.append(jnp.sum(jnp.where(here[:, None, None], merged, 0.0), axis=0))
        placed = jnp.stack(rows)
        if k:
            placed = swap(placed.astype(bf16), GY, lane_count, k).astype(jnp.float32)
        result = placed if result is None else result + placed
    return result


def solution(mesh):
    split = (GX, GY)
    placed = (
        P(split, None, None),
        P(split, None, None, None),
        P(split, None, None, None),
        P(split, None, None),
        P(split, None, None),
        P(split),
        P(split, None),
        P(split, None),
        P(split),
    )
    return jax.shard_map(
        layer, mesh=mesh, in_specs=placed, out_specs=P(split, None, None), check_vma=False
    )
```

```python
import jax
import jax.numpy as jnp
from jax import lax
from jax.experimental import pallas as pl
from jax.experimental.pallas import tpu as pltpu
from jax.sharding import PartitionSpec as P


GX = "gx"
GY = "gy"


def nt(a, b):
    return lax.dot_general(a, b, (((1,), (1,)), ((), ())), preferred_element_type=jnp.float32)


def nn(a, b):
    return jnp.dot(a, b, preferred_element_type=jnp.float32)


def eliminator_of(interp, redinv, pivot_row, rank):
    width, points = interp.shape
    pivot_col = jnp.transpose(jnp.broadcast_to(pivot_row, (8, width)))[:, :1]
    slot = lax.broadcasted_iota(jnp.int32, (width, points), 0)
    point = lax.broadcasted_iota(jnp.int32, (width, points), 1)
    select = jnp.where((point == pivot_col) & (slot < rank), 1.0, 0.0)
    redundant_row = jnp.sum(select, axis=0, keepdims=True) < 0.5
    slot_t = lax.broadcasted_iota(jnp.int32, (points, width), 1)
    point_t = lax.broadcasted_iota(jnp.int32, (points, width), 0)
    select_t = jnp.where((point_t == pivot_row) & (slot_t < rank), 1.0, 0.0)
    redundant_col = jnp.max(select_t, axis=1, keepdims=True) < 0.5
    coefficients = jnp.where((slot < rank) & redundant_row, interp, jnp.zeros_like(interp))
    half_skel = (-nt(redinv, coefficients)).astype(jnp.bfloat16)
    spread = nn(half_skel, select.astype(jnp.bfloat16)).astype(jnp.bfloat16)
    halfway = jnp.where(redundant_row, redinv, spread)
    elim_skel = (-nn(coefficients, halfway)).astype(jnp.bfloat16)
    spread = nn(select_t.astype(jnp.bfloat16), elim_skel).astype(jnp.bfloat16)
    return jnp.where(redundant_col, halfway, spread)


def fill_table(table, neighbors, box_dev, near_count, lane_count, slots):
    me = lax.axis_index(GX)
    for b in range(box_dev):
        for u in range(slots):
            table[b, u] = near_count
    for b in range(box_dev):
        for n in range(near_count):
            target = neighbors[b, n]
            row = target // (box_dev * lane_count)
            table[b, (row ^ me) * box_dev + target % box_dev] = n


def slot_updates(table, slots, elims, back_v, near_v, lifted_v, near_count, group, store, ready=None):
    box_dev, _, width, _ = back_v.shape
    for first in range(0, len(slots), group):
        these = slots[first : first + group]
        for b in range(box_dev):
            rows = jnp.concatenate([back_v[b, table[b, u]] for u in these], axis=0)
            lifted_v[b, pl.ds(0, len(these) * width)] = nn(rows, elims[b][...]).astype(jnp.bfloat16)
        if ready is not None and first == 0:
            ready()
        for i, u in enumerate(these):
            total = None
            for b in range(box_dev):
                if u != b:
                    n = jnp.minimum(table[b, u], near_count - 1)
                    term = nn(lifted_v[b, pl.ds(i * width, width)], near_v[b, n])
                    total = term if total is None else total + term
            store(first + i, (-total).astype(jnp.bfloat16))


def early_kernel(sizes, early):
    box_dev, near_count, lane_count, slots, group = sizes

    def kernel(ranks_h, neighbors_h, pivots_h, interp_h, redinv_h, back_h, near_h, *rest):
        outs, elim_v = rest[:-12], rest[-12]
        ranks, neighbors, pivots, interp_v, redinv_v, back_v, near_v = rest[-11:-4]
        lifted_v, table, few, sems = rest[-4:]
        width, points = interp_v.shape[1:]
        heads = [
            pltpu.make_async_copy(neighbors_h, neighbors, few.at[0]),
            pltpu.make_async_copy(ranks_h, ranks, few.at[1]),
            pltpu.make_async_copy(pivots_h, pivots, few.at[2]),
        ]
        copies = []
        for b in range(box_dev):
            copies.append(
                [
                    pltpu.make_async_copy(interp_h.at[b], interp_v.at[b], sems.at[b, 0]),
                    pltpu.make_async_copy(redinv_h.at[b], redinv_v.at[b], sems.at[b, 1]),
                    pltpu.make_async_copy(
                        back_h.at[b], back_v.at[b, pl.ds(0, near_count)], sems.at[b, 2]
                    ),
                    pltpu.make_async_copy(near_h.at[b], near_v.at[b], sems.at[b, 3]),
                ]
            )
        for copy in heads:
            copy.start()
        for b in range(box_dev):
            copies[b][0].start()
            copies[b][1].start()
        for b in range(box_dev):
            back_v[b, near_count] = jnp.zeros((width, points), jnp.bfloat16)
        for copy in heads:
            copy.wait()
        fill_table(table, neighbors, box_dev, near_count, lane_count, slots)
        elims = []
        for b in range(box_dev):
            copies[b][0].wait()
            copies[b][1].wait()
            if b == 0:
                for j in (2, 3):
                    for c in range(box_dev):
                        copies[c][j].start()
        for b in range(box_dev):
            elim_v[b] = eliminator_of(interp_v[b], redinv_v[b], pivots[pl.ds(b, 1), :], ranks[b])
            elims.append(elim_v.at[b])
        for b in range(box_dev):
            copies[b][2].wait()

        def store(i, block):
            outs[i // group][i % group] = block

        slot_updates(table, early, elims, back_v, near_v, lifted_v, near_count, group, store, lambda: [copies[b][3].wait() for b in range(box_dev)])

    return kernel


def late_kernel(sizes, late):
    box_dev, near_count, lane_count, slots = sizes[:4]

    def kernel(neighbors_h, back_h, near_h, elim_v, *rest):
        outs = rest[:-6]
        neighbors, back_v, near_v, table, few, sems = rest[-6:]
        width, points = back_v.shape[2:]
        head = pltpu.make_async_copy(neighbors_h, neighbors, few.at[0])
        head.start()
        head.wait()
        fill_table(table, neighbors, box_dev, near_count, lane_count, slots)
        copies = []
        for b in range(box_dev):
            for i, u in enumerate(late):
                n = jnp.minimum(table[b, u], near_count - 1)
                copies.append(pltpu.make_async_copy(back_h.at[b, n], back_v.at[b, i], sems.at[0, b, i]))
                copies.append(pltpu.make_async_copy(near_h.at[b, n], near_v.at[b, i], sems.at[1, b, i]))
        for copy in copies:
            copy.start()
        for copy in copies:
            copy.wait()
        lifted = []
        for b in range(box_dev):
            rows = back_v[b].reshape(len(late) * width, points)
            lifted.append(nn(rows, elim_v[b]).astype(jnp.bfloat16))
        for i, u in enumerate(late):
            total = jnp.zeros((width, width), jnp.float32)
            for b in range(box_dev):
                term = nn(lifted[b][i * width : (i + 1) * width], near_v[b, i])
                total += jnp.where(table[b, u] < near_count, term, 0.0)
            outs[i // box_dev][i % box_dev] = (-total).astype(jnp.bfloat16)

    return kernel


def in_hbm(*values):
    return [pltpu.with_memory_space_constraint(v, pltpu.HBM) for v in values]


def swap(value, axis, size, k):
    return lax.ppermute(value, axis, [(a, a ^ k) for a in range(size)])


def layer(self_blk, near, back, interp, redinv, ranks, pivots, neighbors, parent):
    gx_count = lax.axis_size(GX)
    lane_count = lax.axis_size(GY)
    box_dev, near_count, points, width = near.shape
    bf16 = jnp.bfloat16
    half = gx_count // 2
    peers = range(1, half)
    early_k = [k for j in peers for k in (half + j, j)]
    late_k = [half, 0]
    group = 2 * box_dev
    sizes = (box_dev, near_count, lane_count, gx_count * box_dev, group)
    slots_of = lambda ks: [k * box_dev + s for k in ks for s in range(box_dev)]
    hbm = pl.BlockSpec(memory_space=pltpu.HBM)
    vmem = pl.BlockSpec(memory_space=pltpu.VMEM)
    table = pltpu.SMEM((box_dev, gx_count * box_dev), jnp.int32)
    params = pltpu.CompilerParams(vmem_limit_bytes=24 * 1024 * 1024)
    *early, elim = pl.pallas_call(
        early_kernel(sizes, slots_of(early_k)),
        out_shape=[jax.ShapeDtypeStruct((group, width, width), bf16)] * len(peers)
        + [jax.ShapeDtypeStruct((box_dev, points, points), bf16)],
        in_specs=[hbm] * 7,
        out_specs=[vmem] * (len(peers) + 1),
        scratch_shapes=[
            pltpu.SMEM((box_dev,), jnp.int32),
            pltpu.SMEM((box_dev, near_count), jnp.int32),
            pltpu.VMEM((box_dev, width), jnp.int32),
            pltpu.VMEM(interp.shape, bf16),
            pltpu.VMEM(redinv.shape, bf16),
            pltpu.VMEM((box_dev, near_count + 1, width, points), bf16),
            pltpu.VMEM(near.shape, bf16),
            pltpu.VMEM((box_dev, group * width, points), bf16),
            table,
            pltpu.SemaphoreType.DMA((3,)),
            pltpu.SemaphoreType.DMA((box_dev, 4)),
        ],
        compiler_params=params,
        name="early",
    )(*in_hbm(ranks, neighbors, pivots, interp, redinv, back, near))
    joined = [swap(sent, GX, gx_count, j) for j, sent in zip(peers, early)]
    far, close = pl.pallas_call(
        late_kernel(sizes, slots_of(late_k)),
        out_shape=[jax.ShapeDtypeStruct((box_dev, width, width), bf16)] * 2,
        in_specs=[hbm] * 3 + [vmem],
        out_specs=[vmem] * 2,
        scratch_shapes=[
            pltpu.SMEM((box_dev, near_count), jnp.int32),
            pltpu.VMEM((box_dev, len(late_k) * box_dev, width, points), bf16),
            pltpu.VMEM((box_dev, len(late_k) * box_dev, points, width), bf16),
            table,
            pltpu.SemaphoreType.DMA((1,)),
            pltpu.SemaphoreType.DMA((2, box_dev, len(late_k) * box_dev)),
        ],
        compiler_params=params,
        name="late",
    )(*in_hbm(neighbors, back, near), elim)
    joined = [part.astype(jnp.float32) for part in joined]
    far = sum([part[:box_dev] for part in joined], far.astype(jnp.float32)).astype(bf16)
    summed = sum([part[box_dev:] for part in joined], close.astype(jnp.float32))
    summed += swap(far, GX, gx_count, half).astype(jnp.float32)
    living = jnp.arange(width, dtype=jnp.int32)[None, :] < ranks[:, None]
    masking = living[:, :, None] & living[:, None, :]
    merged = jnp.where(masking, self_blk + summed, 0.0)
    row = parent - lax.axis_index(GX) * (lane_count * box_dev)
    lane = lax.axis_index(GY)
    result = None
    for k in range(lane_count):
        rows = []
        for s in range(box_dev):
            here = row == (lane ^ k) * box_dev + s
            rows.append(jnp.sum(jnp.where(here[:, None, None], merged, 0.0), axis=0))
        placed = jnp.stack(rows)
        if k:
            placed = swap(placed.astype(bf16), GY, lane_count, k).astype(jnp.float32)
        result = placed if result is None else result + placed
    return result


def solution(mesh):
    split = (GX, GY)
    placed = (
        P(split, None, None),
        P(split, None, None, None),
        P(split, None, None, None),
        P(split, None, None),
        P(split, None, None),
        P(split),
        P(split, None),
        P(split, None),
        P(split),
    )
    return jax.shard_map(layer, mesh=mesh, in_specs=placed, out_specs=P(split, None, None), check_vma=False)
```

```python
import jax
import jax.numpy as jnp
from jax import lax
from jax.experimental import pallas as pl
from jax.experimental.pallas import tpu as pltpu
from jax.sharding import PartitionSpec as P


GX = "gx"
GY = "gy"


def nt(a, b):
    return lax.dot_general(a, b, (((1,), (1,)), ((), ())), preferred_element_type=jnp.float32)


def nn(a, b):
    return jnp.dot(a, b, preferred_element_type=jnp.float32)


def selections(pivot_row, rank, points):
    width = pivot_row.shape[1]
    pivot_col = jnp.transpose(jnp.broadcast_to(pivot_row, (8, width)))[:, :1]
    slot = lax.broadcasted_iota(jnp.int32, (width, points), 0)
    point = lax.broadcasted_iota(jnp.int32, (width, points), 1)
    select = jnp.where((point == pivot_col) & (slot < rank), 1.0, 0.0)
    redundant_row = jnp.sum(select, axis=0, keepdims=True) < 0.5
    slot_t = lax.broadcasted_iota(jnp.int32, (points, width), 1)
    point_t = lax.broadcasted_iota(jnp.int32, (points, width), 0)
    select_t = jnp.where((point_t == pivot_row) & (slot_t < rank), 1.0, 0.0)
    redundant_col = jnp.max(select_t, axis=1, keepdims=True) < 0.5
    return select.astype(jnp.bfloat16), select_t.astype(jnp.bfloat16), redundant_row, redundant_col


def eliminators_of(interps, redinvs, chosen, ranks):
    boxes = range(len(ranks))
    bf16 = jnp.bfloat16
    select, select_t, redundant_row, redundant_col = zip(*chosen)
    slot = lax.broadcasted_iota(jnp.int32, interps[0].shape, 0)
    coefficients = [
        jnp.where((slot < ranks[b]) & redundant_row[b], interps[b], jnp.zeros_like(interps[b]))
        for b in boxes
    ]
    half_skel = [(-nt(redinvs[b], coefficients[b])).astype(bf16) for b in boxes]
    spread = [nn(half_skel[b], select[b]).astype(bf16) for b in boxes]
    halfway = [jnp.where(redundant_row[b], redinvs[b], spread[b]) for b in boxes]
    elim_skel = [(-nn(coefficients[b], halfway[b])).astype(bf16) for b in boxes]
    spread = [nn(select_t[b], elim_skel[b]).astype(bf16) for b in boxes]
    return [jnp.where(redundant_col[b], halfway[b], spread[b]) for b in boxes]


def fill_table(table, neighbors, box_dev, near_count, lane_count, slots):
    me = lax.axis_index(GX)
    for b in range(box_dev):
        for u in range(slots):
            table[b, u] = near_count
    for b in range(box_dev):
        for n in range(near_count):
            target = neighbors[b, n]
            row = target // (box_dev * lane_count)
            table[b, (row ^ me) * box_dev + target % box_dev] = n


def early_kernel(sizes, early):
    box_dev, near_count, lane_count, slots, group = sizes

    def kernel(ranks_h, neighbors_h, pivots_h, interp_h, redinv_h, back_h, near_h, *rest):
        outs, elim_v = rest[:-12], rest[-12]
        ranks, neighbors, pivots, interp_v, redinv_v, back_v, near_v = rest[-11:-4]
        lifted_v, table, few, sems = rest[-4:]
        width, points = interp_v.shape[1:]
        heads = [
            pltpu.make_async_copy(neighbors_h, neighbors, few.at[0]),
            pltpu.make_async_copy(ranks_h, ranks, few.at[1]),
            pltpu.make_async_copy(pivots_h, pivots, few.at[2]),
        ]
        copies = []
        for b in range(box_dev):
            copies.append(
                [
                    pltpu.make_async_copy(interp_h.at[b], interp_v.at[b], sems.at[b, 0]),
                    pltpu.make_async_copy(redinv_h.at[b], redinv_v.at[b], sems.at[b, 1]),
                    pltpu.make_async_copy(
                        back_h.at[b], back_v.at[b, pl.ds(0, near_count)], sems.at[b, 2]
                    ),
                    pltpu.make_async_copy(near_h.at[b], near_v.at[b], sems.at[b, 3]),
                ]
            )
        for copy in heads:
            copy.start()
        for b in range(box_dev):
            copies[b][0].start()
            copies[b][1].start()

        def lift(b):
            for first in range(0, len(early), 16):
                some = early[first : first + 16]
                rows = jnp.concatenate([back_v[b, table[b, u]] for u in some], axis=0)
                span = pl.ds(first * width, len(some) * width)
                lifted_v[b, span] = nn(rows, elim_v[b]).astype(jnp.bfloat16)

        def update(i):
            total = None
            for b in range(box_dev):
                n = jnp.minimum(table[b, early[i]], near_count - 1)
                term = nn(lifted_v[b, pl.ds(i * width, width)], near_v[b, n])
                total = term if total is None else total + term
            outs[i // group][i % group] = (-total).astype(jnp.bfloat16)

        def start(j, boxes):
            for b in boxes:
                copies[b][j].start()

        def wait(j, boxes):
            for b in boxes:
                copies[b][j].wait()

        boxes = range(box_dev)
        for b in range(box_dev):
            back_v[b, near_count] = jnp.zeros((width, points), jnp.bfloat16)
        for copy in heads:
            copy.wait()
        wait(0, boxes[:1])
        wait(1, boxes[:1])
        start(2, boxes)
        fill_table(table, neighbors, box_dev, near_count, lane_count, slots)
        wait(0, boxes[1:])
        wait(1, boxes[1:])
        start(3, boxes)
        chosen = [selections(pivots[pl.ds(b, 1), :], ranks[b], points) for b in boxes]
        made = eliminators_of(
            [interp_v[b] for b in boxes], [redinv_v[b] for b in boxes], chosen, [ranks[b] for b in boxes]
        )
        for b in boxes:
            elim_v[b] = made[b]
        wait(2, boxes)
        for b in boxes:
            lift(b)
        wait(3, boxes)
        for i in range(len(early)):
            update(i)

    return kernel


def late_kernel(sizes, late):
    box_dev, near_count, lane_count, slots = sizes[:4]

    def kernel(neighbors_h, back_h, near_h, elim_v, *rest):
        outs = rest[:-6]
        neighbors, back_v, near_v, table, few, sems = rest[-6:]
        width, points = back_v.shape[2:]
        head = pltpu.make_async_copy(neighbors_h, neighbors, few.at[0])
        head.start()
        head.wait()
        fill_table(table, neighbors, box_dev, near_count, lane_count, slots)
        copies = []
        for b in range(box_dev):
            for i, u in enumerate(late):
                n = jnp.minimum(table[b, u], near_count - 1)
                for side, (source, target) in enumerate(((back_h, back_v), (near_h, near_v))):
                    copies.append(
                        pltpu.make_async_copy(
                            source.at[b, n], target.at[b, i], sems.at[side, b, i]
                        )
                    )
        for copy in copies:
            copy.start()
        for copy in copies:
            copy.wait()
        lifted = []
        for b in range(box_dev):
            rows = back_v[b].reshape(len(late) * width, points)
            lifted.append(nn(rows, elim_v[b]).astype(jnp.bfloat16))
        for i, u in enumerate(late):
            total = jnp.zeros((width, width), jnp.float32)
            for b in range(box_dev):
                term = nn(lifted[b][i * width : (i + 1) * width], near_v[b, i])
                total += jnp.where(table[b, u] < near_count, term, 0.0)
            outs[i // box_dev][i % box_dev] = (-total).astype(jnp.bfloat16)

    return kernel


def in_hbm(*values):
    return [pltpu.with_memory_space_constraint(v, pltpu.HBM) for v in values]


def swap(value, axis, size, k):
    return lax.ppermute(value, axis, [(a, a ^ k) for a in range(size)])


def layer(self_blk, near, back, interp, redinv, ranks, pivots, neighbors, parent):
    gx_count = lax.axis_size(GX)
    lane_count = lax.axis_size(GY)
    box_dev, near_count, points, width = near.shape
    bf16 = jnp.bfloat16
    half = gx_count // 2
    peers = range(1, half)
    early_k = [k for j in peers for k in (half + j, j)]
    late_k = [half, 0]
    group = 2 * box_dev
    sizes = (box_dev, near_count, lane_count, gx_count * box_dev, group)
    slots_of = lambda ks: [k * box_dev + s for k in ks for s in range(box_dev)]
    hbm = pl.BlockSpec(memory_space=pltpu.HBM)
    vmem = pl.BlockSpec(memory_space=pltpu.VMEM)
    table = pltpu.SMEM((box_dev, gx_count * box_dev), jnp.int32)
    params = pltpu.CompilerParams(vmem_limit_bytes=48 * 1024 * 1024)
    *early, elim = pl.pallas_call(
        early_kernel(sizes, slots_of(early_k)),
        out_shape=[jax.ShapeDtypeStruct((group, width, width), bf16)] * len(peers)
        + [jax.ShapeDtypeStruct((box_dev, points, points), bf16)],
        in_specs=[hbm] * 7,
        out_specs=[vmem] * (len(peers) + 1),
        scratch_shapes=[
            pltpu.SMEM((box_dev,), jnp.int32),
            pltpu.SMEM((box_dev, near_count), jnp.int32),
            pltpu.VMEM((box_dev, width), jnp.int32),
            pltpu.VMEM(interp.shape, bf16),
            pltpu.VMEM(redinv.shape, bf16),
            pltpu.VMEM((box_dev, near_count + 1, width, points), bf16),
            pltpu.VMEM(near.shape, bf16),
            pltpu.VMEM((box_dev, len(early_k) * box_dev * width, points), bf16),
            table,
            pltpu.SemaphoreType.DMA((3,)),
            pltpu.SemaphoreType.DMA((box_dev, 4)),
        ],
        compiler_params=params,
        name="early",
    )(*in_hbm(ranks, neighbors, pivots, interp, redinv, back, near))
    joined = [swap(sent, GX, gx_count, j) for j, sent in zip(peers, early)]
    far, close = pl.pallas_call(
        late_kernel(sizes, slots_of(late_k)),
        out_shape=[jax.ShapeDtypeStruct((box_dev, width, width), bf16)] * 2,
        in_specs=[hbm] * 3 + [vmem],
        out_specs=[vmem] * 2,
        scratch_shapes=[
            pltpu.SMEM((box_dev, near_count), jnp.int32),
            pltpu.VMEM((box_dev, len(late_k) * box_dev, width, points), bf16),
            pltpu.VMEM((box_dev, len(late_k) * box_dev, points, width), bf16),
            table,
            pltpu.SemaphoreType.DMA((1,)),
            pltpu.SemaphoreType.DMA((2, box_dev, len(late_k) * box_dev)),
        ],
        compiler_params=params,
        name="late",
    )(*in_hbm(neighbors, back, near), elim)
    joined = [part.astype(jnp.float32) for part in joined]
    far = sum([part[:box_dev] for part in joined], far.astype(jnp.float32)).astype(bf16)
    summed = sum([part[box_dev:] for part in joined], close.astype(jnp.float32))
    summed += swap(far, GX, gx_count, half).astype(jnp.float32)
    living = jnp.arange(width, dtype=jnp.int32)[None, :] < ranks[:, None]
    masking = living[:, :, None] & living[:, None, :]
    merged = jnp.where(masking, self_blk + summed, 0.0)
    row = parent - lax.axis_index(GX) * (lane_count * box_dev)
    lane = lax.axis_index(GY)
    result = None
    for k in range(lane_count):
        rows = []
        for s in range(box_dev):
            here = row == (lane ^ k) * box_dev + s
            rows.append(jnp.sum(jnp.where(here[:, None, None], merged, 0.0), axis=0))
        placed = jnp.stack(rows)
        if k:
            placed = swap(placed.astype(bf16), GY, lane_count, k).astype(jnp.float32)
        result = placed if result is None else result + placed
    return result


def solution(mesh):
    split = (GX, GY)
    placed = (
        P(split, None, None),
        P(split, None, None, None),
        P(split, None, None, None),
        P(split, None, None),
        P(split, None, None),
        P(split),
        P(split, None),
        P(split, None),
        P(split),
    )
    return jax.shard_map(
        layer, mesh=mesh, in_specs=placed, out_specs=P(split, None, None), check_vma=False
    )
```

```python
import jax
import jax.numpy as jnp
from jax import lax
from jax.experimental import pallas as pl
from jax.experimental.pallas import tpu as pltpu
from jax.sharding import PartitionSpec as P


GX = "gx"
GY = "gy"


def nt(a, b):
    return lax.dot_general(a, b, (((1,), (1,)), ((), ())), preferred_element_type=jnp.float32)


def nn(a, b):
    return jnp.dot(a, b, preferred_element_type=jnp.float32)


def selections(pivot_row, rank, points):
    bf16 = jnp.bfloat16
    width = pivot_row.shape[1]
    pivot_col = jnp.transpose(jnp.broadcast_to(pivot_row, (8, width)))[:, :1]
    slot = lax.broadcasted_iota(jnp.int32, (width, points), 0)
    point = lax.broadcasted_iota(jnp.int32, (width, points), 1)
    select = jnp.where((point == pivot_col) & (slot < rank), 1.0, 0.0)
    redundant_row = 1.0 - jnp.sum(select, axis=0, keepdims=True)
    slot_t = lax.broadcasted_iota(jnp.int32, (points, width), 1)
    point_t = lax.broadcasted_iota(jnp.int32, (points, width), 0)
    minus_t = jnp.where((point_t == pivot_row) & (slot_t < rank), -1.0, 0.0)
    redundant_col = 1.0 + jnp.min(minus_t, axis=1, keepdims=True)
    alive = jnp.where(slot[:, :1] < rank, -1.0, 0.0)
    return (
        select.astype(bf16),
        minus_t.astype(bf16),
        redundant_row.astype(bf16),
        redundant_col.astype(bf16),
        alive.astype(bf16),
    )


def eliminators_of(interps, redinvs, chosen):
    boxes = range(len(interps))
    bf16 = jnp.bfloat16
    select, minus_t, redundant_row, redundant_col, alive = zip(*chosen)
    minus_c = [interps[b] * alive[b] * redundant_row[b] for b in boxes]
    half_skel = [nt(redinvs[b], minus_c[b]).astype(bf16) for b in boxes]
    spread = [nn(half_skel[b], select[b]).astype(bf16) for b in boxes]
    halfway = [redinvs[b] * redundant_row[b] + spread[b] for b in boxes]
    elim_skel = [nn(minus_c[b], halfway[b]).astype(bf16) for b in boxes]
    spread = [nn(minus_t[b], elim_skel[b]).astype(bf16) for b in boxes]
    return [spread[b] - halfway[b] * redundant_col[b] for b in boxes]


def fill_table(table, neighbors, box_dev, near_count, lane_count, slots):
    me = lax.axis_index(GX)
    for b in range(box_dev):
        for u in range(slots):
            table[b, u] = near_count
    for b in range(box_dev):
        for n in range(near_count):
            target = neighbors[b, n]
            row = target // (box_dev * lane_count)
            table[b, (row ^ me) * box_dev + target % box_dev] = n


def early_kernel(sizes, early):
    box_dev, near_count, lane_count, slots, group = sizes

    def kernel(ranks_h, neighbors_h, pivots_h, interp_h, redinv_h, back_h, near_h, *rest):
        outs, elim_v = rest[:-12], rest[-12]
        ranks, neighbors, pivots, interp_v, redinv_v, back_v, near_v = rest[-11:-4]
        lifted_v, table, few, sems = rest[-4:]
        width, points = interp_v.shape[1:]
        heads = [
            pltpu.make_async_copy(neighbors_h, neighbors, few.at[0]),
            pltpu.make_async_copy(ranks_h, ranks, few.at[1]),
            pltpu.make_async_copy(pivots_h, pivots, few.at[2]),
        ]
        copies = []
        for b in range(box_dev):
            copies.append(
                [
                    pltpu.make_async_copy(interp_h.at[b], interp_v.at[b], sems.at[b, 0]),
                    pltpu.make_async_copy(redinv_h.at[b], redinv_v.at[b], sems.at[b, 1]),
                    pltpu.make_async_copy(
                        back_h.at[b], back_v.at[b, pl.ds(0, near_count)], sems.at[b, 2]
                    ),
                    pltpu.make_async_copy(near_h.at[b], near_v.at[b], sems.at[b, 3]),
                ]
            )
        for copy in heads:
            copy.start()
        for b in range(box_dev):
            copies[b][0].start()
            copies[b][1].start()

        def lift(b):
            for first in range(0, len(early), 16):
                some = early[first : first + 16]
                rows = jnp.concatenate([back_v[b, table[b, u]] for u in some], axis=0)
                span = pl.ds(first * width, len(some) * width)
                lifted_v[b, span] = nn(rows, elim_v[b]).astype(jnp.bfloat16)

        def update(i):
            total = None
            for b in range(box_dev):
                n = jnp.minimum(table[b, early[i]], near_count - 1)
                term = nn(lifted_v[b, pl.ds(i * width, width)], near_v[b, n])
                total = term if total is None else total + term
            outs[i // group][i % group] = total.astype(jnp.bfloat16)

        def start(j, boxes):
            for b in boxes:
                copies[b][j].start()

        def wait(j, boxes):
            for b in boxes:
                copies[b][j].wait()

        boxes = range(box_dev)
        for b in range(box_dev):
            back_v[b, near_count] = jnp.zeros((width, points), jnp.bfloat16)
        for copy in heads:
            copy.wait()
        wait(0, boxes[:1])
        wait(1, boxes[:1])
        start(2, boxes)
        fill_table(table, neighbors, box_dev, near_count, lane_count, slots)
        wait(0, boxes[1:])
        wait(1, boxes[1:])
        start(3, boxes)
        chosen = [selections(pivots[pl.ds(b, 1), :], ranks[b], points) for b in boxes]
        made = eliminators_of(
            [interp_v[b] for b in boxes], [redinv_v[b] for b in boxes], chosen
        )
        for b in boxes:
            elim_v[b] = made[b]
        for b in boxes:
            wait(2, [b])
            lift(b)
        wait(3, boxes)
        for i in range(len(early)):
            update(i)

    return kernel


def late_kernel(sizes, late):
    box_dev, near_count, lane_count, slots = sizes[:4]

    def kernel(neighbors_h, back_h, near_h, elim_v, *rest):
        outs = rest[:-6]
        neighbors, back_v, near_v, table, few, sems = rest[-6:]
        width, points = back_v.shape[2:]
        head = pltpu.make_async_copy(neighbors_h, neighbors, few.at[0])
        head.start()
        head.wait()
        fill_table(table, neighbors, box_dev, near_count, lane_count, slots)
        copies = []
        for b in range(box_dev):
            for i, u in enumerate(late):
                n = jnp.minimum(table[b, u], near_count - 1)
                for side, (source, target) in enumerate(((back_h, back_v), (near_h, near_v))):
                    copies.append(
                        pltpu.make_async_copy(
                            source.at[b, n], target.at[b, i], sems.at[side, b, i]
                        )
                    )
        for copy in copies:
            copy.start()
        for copy in copies:
            copy.wait()
        lifted = []
        for b in range(box_dev):
            rows = back_v[b].reshape(len(late) * width, points)
            lifted.append(nn(rows, elim_v[b]).astype(jnp.bfloat16))
        for i, u in enumerate(late):
            total = jnp.zeros((width, width), jnp.float32)
            for b in range(box_dev):
                term = nn(lifted[b][i * width : (i + 1) * width], near_v[b, i])
                total += jnp.where(table[b, u] < near_count, term, 0.0)
            outs[i // box_dev][i % box_dev] = total.astype(jnp.bfloat16)

    return kernel


def in_hbm(*values):
    return [pltpu.with_memory_space_constraint(v, pltpu.HBM) for v in values]


def swap(value, axis, size, k):
    return lax.ppermute(value, axis, [(a, a ^ k) for a in range(size)])


def layer(self_blk, near, back, interp, redinv, ranks, pivots, neighbors, parent):
    gx_count = lax.axis_size(GX)
    lane_count = lax.axis_size(GY)
    box_dev, near_count, points, width = near.shape
    bf16 = jnp.bfloat16
    half = gx_count // 2
    peers = range(1, half)
    early_k = [k for j in peers for k in (half + j, j)]
    late_k = [half, 0]
    group = 2 * box_dev
    sizes = (box_dev, near_count, lane_count, gx_count * box_dev, group)
    slots_of = lambda ks: [k * box_dev + s for k in ks for s in range(box_dev)]
    hbm = pl.BlockSpec(memory_space=pltpu.HBM)
    vmem = pl.BlockSpec(memory_space=pltpu.VMEM)
    table = pltpu.SMEM((box_dev, gx_count * box_dev), jnp.int32)
    params = pltpu.CompilerParams(vmem_limit_bytes=48 * 1024 * 1024)
    *early, elim = pl.pallas_call(
        early_kernel(sizes, slots_of(early_k)),
        out_shape=[jax.ShapeDtypeStruct((group, width, width), bf16)] * len(peers)
        + [jax.ShapeDtypeStruct((box_dev, points, points), bf16)],
        in_specs=[hbm] * 7,
        out_specs=[vmem] * (len(peers) + 1),
        scratch_shapes=[
            pltpu.SMEM((box_dev,), jnp.int32),
            pltpu.SMEM((box_dev, near_count), jnp.int32),
            pltpu.VMEM((box_dev, width), jnp.int32),
            pltpu.VMEM(interp.shape, bf16),
            pltpu.VMEM(redinv.shape, bf16),
            pltpu.VMEM((box_dev, near_count + 1, width, points), bf16),
            pltpu.VMEM(near.shape, bf16),
            pltpu.VMEM((box_dev, len(early_k) * box_dev * width, points), bf16),
            table,
            pltpu.SemaphoreType.DMA((3,)),
            pltpu.SemaphoreType.DMA((box_dev, 4)),
        ],
        compiler_params=params,
        name="early",
    )(*in_hbm(ranks, neighbors, pivots, interp, redinv, back, near))
    joined = [swap(sent, GX, gx_count, j) for j, sent in zip(peers, early)]
    far, close = pl.pallas_call(
        late_kernel(sizes, slots_of(late_k)),
        out_shape=[jax.ShapeDtypeStruct((box_dev, width, width), bf16)] * 2,
        in_specs=[hbm] * 3 + [vmem],
        out_specs=[vmem] * 2,
        scratch_shapes=[
            pltpu.SMEM((box_dev, near_count), jnp.int32),
            pltpu.VMEM((box_dev, len(late_k) * box_dev, width, points), bf16),
            pltpu.VMEM((box_dev, len(late_k) * box_dev, points, width), bf16),
            table,
            pltpu.SemaphoreType.DMA((1,)),
            pltpu.SemaphoreType.DMA((2, box_dev, len(late_k) * box_dev)),
        ],
        compiler_params=params,
        name="late",
    )(*in_hbm(neighbors, back, near), elim)
    joined = [part.astype(jnp.float32) for part in joined]
    far = sum([part[:box_dev] for part in joined], far.astype(jnp.float32)).astype(bf16)
    summed = sum([part[box_dev:] for part in joined], close.astype(jnp.float32))
    summed += swap(far, GX, gx_count, half).astype(jnp.float32)
    living = jnp.arange(width, dtype=jnp.int32)[None, :] < ranks[:, None]
    masking = living[:, :, None] & living[:, None, :]
    merged = jnp.where(masking, self_blk + summed, 0.0)
    row = parent - lax.axis_index(GX) * (lane_count * box_dev)
    lane = lax.axis_index(GY)
    result = None
    for k in range(lane_count):
        rows = []
        for s in range(box_dev):
            here = row == (lane ^ k) * box_dev + s
            rows.append(jnp.sum(jnp.where(here[:, None, None], merged, 0.0), axis=0))
        placed = jnp.stack(rows)
        if k:
            placed = swap(placed.astype(bf16), GY, lane_count, k).astype(jnp.float32)
        result = placed if result is None else result + placed
    return result


def solution(mesh):
    split = (GX, GY)
    placed = (
        P(split, None, None),
        P(split, None, None, None),
        P(split, None, None, None),
        P(split, None, None),
        P(split, None, None),
        P(split),
        P(split, None),
        P(split, None),
        P(split),
    )
    return jax.shard_map(
        layer, mesh=mesh, in_specs=placed, out_specs=P(split, None, None), check_vma=False
    )
```
